256 devices in a mesh: dp: 4 (over x), expert: 64 (over z, y, core).
Axes of the slice: x: 4, y: 4, z: 8, core: 2. Of those that a mesh axis runs over, the one named last changes fastest.
Arguments:
- tokens: bfloat16 [4096, 4096], P(('dp', 'expert')), may hold values from -6 to 6
- expert_ids: int32 [4096, 8], P(('dp', 'expert')), may hold values from 0 to 127, all different within a row
- scores: float32 [4096, 8], P(('dp', 'expert')), may hold values from 0.05 to 1
- up_weight: bfloat16 [128, 4096, 1024], P('expert', 'dp'), may hold values from -0.09375 to 0.09375
- down_weight: bfloat16 [128, 1024, 4096], P('expert', None, 'dp'), may hold values from -0.1875 to 0.1875
- swap_slot: int32 [64], replicated, may hold values from 0 to 2, as said below
Outputs:
- combined: bfloat16 [4096, 4096], P(('dp', 'expert'))
The draws below stay inside these ranges and needn't reach their ends.
Inputs may be any that keep to these rules, and one draw needn't show every extreme that they name: `swap_slot`: the value 2 means that the index gives no slot; indices i and (i + 32) mod 64 both give a slot below 2 or both have 2.
All inputs are finite; a program needn't handle non-finite values.
Results may differ from the reference program's by a relative error of at most 0.0058.
Values may be sent and summed in bfloat16 or wider, within the bound.
No kernel may reach another device: no remote copies, remote signals or barrier semaphores. Data moves between devices by JAX's collectives and lax.ppermute only.
A program may use at most 64 MiB of HBM per device.

```python
import math
import jax
import jax.numpy as jnp
from jax import lax

D = 4096
FF = 1024
EXP_DEV = 2
TOP = 8
CAP_SLOTS = 2
HOLD_CAP = 3
TOK_DEV = 16
HOLDERS = 64
EXPERTS = 128
TOKENS = 4096


def draw_swap_slot(key, part):
    first, second = jax.random.split(jax.random.fold_in(key, 17))
    flags = jax.random.randint(first, (HOLDERS // 2,), 0, 4)
    flags = flags.at[0].set(0).at[1].set(3)
    slot_pick = jax.random.randint(second, (HOLDERS,), 0, EXP_DEV)
    paired = jnp.concatenate([flags, flags])
    return jnp.where(paired < 3, slot_pick, EXP_DEV).astype(jnp.int32)


def block_levels(stream_key, dims, cuts, low, high):
    level, own = 1.0, jax.random.fold_in(stream_key, 6)
    for dim, parts in cuts:
        steps = jnp.exp(jax.random.uniform(jax.random.fold_in(own, dim), (parts,), jnp.float32, low / len(cuts), high / len(cuts)))
        level = level * jnp.repeat(steps, dims[dim] // parts).reshape([-1 if axis == dim else 1 for axis in range(len(dims))])
    return level


def picks_of(key, rows, amount, top, lift):
    order = jax.random.permutation(jax.random.fold_in(key, 1), amount)
    favour = order
    for power in range(3):
        favour = favour * favour // amount
    favour = favour * lift // amount
    chance = jax.random.randint(jax.random.fold_in(key, 2), (rows, amount), 0, 4096) + favour
    fixed_rows = jax.random.permutation(jax.random.fold_in(key, 3), rows)[jnp.arange(amount) % rows]
    chance = jnp.where(jnp.arange(rows)[:, None] == fixed_rows[None, :], 1 << 14, chance)
    score = chance * amount + jnp.arange(amount)
    return lax.top_k(score.astype(jnp.int32), top)[1].astype(jnp.int32)


def bell_draw(rng, extent, spread, bound, cuts=(), kind=jnp.bfloat16):
    level = block_levels(rng, extent, cuts, -0.22, 0.18) if cuts else 1.0
    result = jax.random.normal(rng, extent, jnp.float32) * spread * level
    return jnp.minimum(jnp.maximum(result, -bound), bound).astype(kind)


def setup_inputs(seed: int = 0) -> dict:
    seeds = jax.random.split(jax.random.key(seed), 7)
    tokens = bell_draw(seeds[0], (TOKENS, D), 1.0, 6.0, ((0, 256),))
    expert_ids = picks_of(seeds[1], TOKENS, EXPERTS, TOP, 1024)
    scores = jnp.clip(jnp.exp(math.log(1.0) - 2.9957323 * jax.random.uniform(seeds[2], (TOKENS, TOP), jnp.float32) ** block_levels(seeds[2], (TOKENS, TOP), ((0, 256),), -0.2, 0.2)), 0.05, 1.0)
    up_weight = bell_draw(seeds[3], (EXPERTS, D, FF), D ** -0.5, 0.09375, ((0, 64), (1, 4)))
    down_weight = bell_draw(seeds[4], (EXPERTS, FF, D), FF ** -0.5, 0.1875, ((0, 64), (2, 4)))
    swap_slot = draw_swap_slot(jax.random.fold_in(seeds[6], 71), 0)
    return dict(tokens=tokens, expert_ids=expert_ids, scores=scores, up_weight=up_weight, down_weight=down_weight, swap_slot=swap_slot)


row_block = 128


def block_rank(keys):
    same_key = keys[:, :, None] == keys[:, None, :]
    positions = jnp.arange(keys.shape[1], dtype=jnp.int32)
    earlier = positions[None, :] < positions[:, None]
    return jnp.sum(jnp.where(same_key & earlier[None], 1, 0), axis=2).astype(jnp.int32)


def reference(tokens, expert_ids, scores, up_weight, down_weight, swap_slot):
    experts_all = jnp.arange(EXPERTS, dtype=jnp.int32)
    home_device = experts_all // EXP_DEV
    home_slot = experts_all % EXP_DEV
    partner = (home_device + HOLDERS // 2) % HOLDERS
    relocated = swap_slot[home_device] == home_slot
    holder = jnp.where(relocated, partner, home_device).astype(jnp.int32)
    per_dev = TOK_DEV * TOP
    flat_ids = expert_ids.reshape(-1).astype(jnp.int32)
    target = holder[flat_ids].reshape(-1, per_dev)
    holder_rank = block_rank(target)
    expert_rank = block_rank(flat_ids.reshape(-1, per_dev))
    kept_mask = ((holder_rank < HOLD_CAP) & (expert_rank < CAP_SLOTS)).reshape(-1)
    gate_share = 2.5 * scores / jnp.sum(scores, axis=1, keepdims=True)
    weight_flat = jnp.where(kept_mask, gate_share.reshape(-1), jnp.zeros_like(gate_share.reshape(-1)))
    sort_key = jnp.where(kept_mask, flat_ids, EXPERTS).astype(jnp.int32)
    ordering = jnp.argsort(sort_key, stable=True).astype(jnp.int32)
    counts = jnp.sum((sort_key[:, None] == experts_all[None, :]).astype(jnp.int32), axis=0).astype(jnp.int32)
    offsets = (jnp.cumsum(counts) - counts).astype(jnp.int32)
    padded = jnp.concatenate([ordering, jnp.zeros((row_block,), jnp.int32)])
    accum_start = jnp.zeros(tokens.shape, jnp.float32)

    def per_expert(expert, accum):
        begin = offsets[expert]
        number = counts[expert]
        up_matrix = lax.dynamic_index_in_dim(up_weight, expert, 0, keepdims=False)
        down_matrix = lax.dynamic_index_in_dim(down_weight, expert, 0, keepdims=False)

        def blocks_left(loop_state):
            return loop_state[0] * row_block < number

        def advance(loop_state):
            block_idx, running = loop_state
            picked = lax.dynamic_slice_in_dim(padded, (begin + block_idx * row_block).astype(jnp.int32), row_block)
            valid_rows = jnp.arange(row_block, dtype=jnp.int32) + block_idx * row_block < number
            token_rows = picked // TOP
            gathered = tokens[token_rows]
            hidden = jax.nn.silu(jnp.dot(gathered, up_matrix, preferred_element_type=jnp.float32)).astype(jnp.bfloat16)
            expert_out = jnp.dot(hidden, down_matrix, preferred_element_type=jnp.float32).astype(jnp.bfloat16)
            scaled = jnp.where(valid_rows, weight_flat[picked], jnp.zeros_like(weight_flat[picked]))
            running = running.at[token_rows].add(scaled[:, None] * expert_out.astype(jnp.float32))
            return block_idx + 1, running

        return lax.while_loop(blocks_left, advance, (jnp.int32(0), accum))[1]

    accum = lax.fori_loop(0, EXPERTS, per_expert, accum_start)
    return accum.astype(jnp.bfloat16)
```

```python
import jax
import jax.numpy as jnp
from jax import lax
from jax.sharding import Mesh, PartitionSpec as P

CAP_SLOTS = 2
HOLD_CAP = 3
BF = jnp.bfloat16
F32 = jnp.float32


def slot_weights(expert_ids, scores, swap_slot, experts):
    tok_rows, chosen = expert_ids.shape
    holders = swap_slot.shape[0]
    per_dev = experts // holders
    ids = jnp.arange(experts, dtype=jnp.int32)
    home = ids // per_dev
    swap_of = jnp.broadcast_to(swap_slot[:, None], (holders, per_dev)).reshape(experts)
    holder = jnp.where(swap_of == ids % per_dev, (home + holders // 2) % holders, home)
    picks = expert_ids[:, :, None] == ids[None, None, :]
    order = jnp.arange(1, chosen + 1, dtype=jnp.int32)[None, :, None]
    place = jnp.sum(jnp.where(picks, order, 0), axis=1)
    gate = 2.5 * scores / jnp.sum(scores, axis=1, keepdims=True)
    share = jnp.sum(jnp.where(picks, gate[:, :, None], 0.0), axis=1)
    picked = place > 0
    same = holder[:, None] == holder[None, :]
    mate = same & (ids[:, None] != ids[None, :])
    before = jnp.tril(jnp.ones((tok_rows, tok_rows), F32), -1)
    ones = picked.astype(F32)
    in_rows = jnp.dot(ones, same.astype(F32))
    mate_place = jnp.dot(place.astype(F32), mate.astype(F32))
    earlier = (mate_place > 0) & (mate_place < place.astype(F32))
    holder_rank = jnp.dot(before, in_rows) + earlier.astype(F32)
    expert_rank = jnp.dot(before, ones)
    kept = picked & (holder_rank < HOLD_CAP)
    return [jnp.where(kept & (expert_rank == rank), share, 0.0) for rank in range(CAP_SLOTS)]


def body(tokens, expert_ids, scores, up_weight, down_weight, swap_slot):
    groups = lax.axis_size("dp")
    planes = lax.axis_size("z")
    cells = lax.axis_size("yc")
    tok_rows, width = tokens.shape
    per_dev = up_weight.shape[0]
    experts = planes * cells * per_dev
    part_width = width // groups
    blocks = groups * planes
    plane_experts = cells * per_dev
    weights = slot_weights(expert_ids, scores, swap_slot, experts)
    high = [lax.reduce_precision(w, 8, 7) for w in weights]
    low = [w - h for w, h in zip(weights, high)]
    meta = jnp.stack(high + low, axis=1).astype(BF)
    meta = meta.reshape(tok_rows, 2 * CAP_SLOTS, planes, plane_experts).transpose(2, 0, 1, 3)
    meta_used = 2 * CAP_SLOTS * plane_experts
    meta = meta.reshape(planes, tok_rows, meta_used)
    meta_cols = -(-meta_used // 128) * 128
    meta = jnp.pad(meta, ((0, 0), (0, 0), (0, meta_cols - meta_used)))
    feats = tokens.reshape(tok_rows, groups, part_width).transpose(1, 0, 2)
    payload = jnp.concatenate(
        [
            jnp.broadcast_to(feats[:, None], (groups, planes, tok_rows, part_width)),
            jnp.broadcast_to(meta[None], (groups, planes, tok_rows, meta_cols)),
        ],
        axis=-1,
    ).reshape(blocks, tok_rows, part_width + meta_cols)
    spread = lax.all_to_all(payload, ("dp", "z"), 0, 0, tiled=True)
    spread = spread.reshape(blocks * tok_rows, part_width + meta_cols)
    tok = spread[:, :part_width]
    info = spread[:, part_width:]
    cell_rows = CAP_SLOTS * blocks
    slots = cells * cell_rows
    slot = jnp.arange(slots, dtype=jnp.int32)
    slot_cell = slot // cell_rows
    slot_rank = (slot % cell_rows) // blocks
    slot_block = slot % blocks
    own = (jnp.arange(blocks * tok_rows, dtype=jnp.int32) // tok_rows)[:, None] == slot_block[None, :]
    columns = jnp.arange(meta_cols, dtype=jnp.int32)[:, None]
    total = jnp.zeros((blocks * tok_rows, part_width), F32)
    for s in range(per_dev):
        source = slot_rank * plane_experts + slot_cell * per_dev + s
        pick_high = (columns == source[None, :]).astype(BF)
        pick_low = (columns == source[None, :] + CAP_SLOTS * plane_experts).astype(BF)
        spread_high = jnp.where(own, jnp.dot(info, pick_high, preferred_element_type=F32), 0.0).astype(BF)
        spread_low = jnp.where(own, jnp.dot(info, pick_low, preferred_element_type=F32), 0.0).astype(BF)
        rows = lax.dot_general(
            (spread_high > 0).astype(BF), tok, (((0,), (0,)), ((), ())), preferred_element_type=F32
        ).astype(BF)
        arrived = lax.all_to_all(rows.reshape(cells, cell_rows, part_width), "yc", 0, 0, tiled=True)
        arrived = arrived.reshape(slots, part_width)
        terms = jnp.dot(arrived, up_weight[s], preferred_element_type=F32).astype(BF)
        hidden_width = terms.shape[1]
        shares = lax.all_to_all(terms.reshape(groups, slots // groups, hidden_width), "dp", 0, 0, tiled=True)
        hidden = jax.nn.silu(jnp.sum(shares.astype(F32), axis=0)).astype(BF)
        copies = jnp.broadcast_to(hidden[None], (groups,) + hidden.shape)
        whole = lax.all_to_all(copies, "dp", 0, 0, tiled=True).reshape(slots, hidden_width)
        result = jnp.dot(whole, down_weight[s], preferred_element_type=F32).astype(BF)
        back = lax.all_to_all(result.reshape(cells, cell_rows, part_width), "yc", 0, 0, tiled=True)
        back = back.reshape(slots, part_width)
        total = total + jnp.dot(spread_high, back, preferred_element_type=F32)
        total = total + jnp.dot(spread_low, back, preferred_element_type=F32)
    sums = total.astype(BF).reshape(blocks, tok_rows, part_width)
    parts = lax.all_to_all(sums, ("dp", "z"), 0, 0, tiled=True)
    parts = jnp.sum(parts.reshape(groups, planes, tok_rows, part_width).astype(F32), axis=1)
    return parts.astype(BF).transpose(1, 0, 2).reshape(tok_rows, width)


def solution(mesh):
    groups, holders = mesh.devices.shape
    cells = 8 if holders % 8 == 0 else holders
    grid = Mesh(mesh.devices.reshape(groups, holders // cells, cells), ("dp", "z", "yc"))
    every = ("dp", "z", "yc")
    return jax.shard_map(
        body,
        mesh=grid,
        in_specs=(
            P(every, None),
            P(every, None),
            P(every, None),
            P(("z", "yc"), "dp", None),
            P(("z", "yc"), None, "dp"),
            P(),
        ),
        out_specs=P(every, None),
        check_vma=False,
    )
```

```python
import functools

import jax
import jax.numpy as jnp
from jax import lax
from jax.experimental import pallas as pl
from jax.experimental.pallas import tpu as pltpu
from jax.sharding import Mesh, PartitionSpec as P

CAP_SLOTS = 2
HOLD_CAP = 3
META_COLS = 128
TILE = 512
VMEM_LIMIT = 16 << 20
BF = jnp.bfloat16
F32 = jnp.float32
I32 = jnp.int32


def iota(shape, dim):
    return lax.broadcasted_iota(I32, shape, dim)


def shift(value, axis, steps):
    count = lax.axis_size(axis)
    return lax.ppermute(value, axis, [(source, (source + steps) % count) for source in range(count)])


def local_call(kernel, inputs, outputs, scalars=(), hbm=(), scratch=(), flops=0):
    moved = sum(a.size * a.dtype.itemsize for a in [*hbm, *inputs, *outputs])
    vmem = pl.BlockSpec(memory_space=pltpu.VMEM)
    return pl.pallas_call(
        kernel,
        in_specs=[pl.BlockSpec(memory_space=pltpu.SMEM)] * len(scalars)
        + [pl.BlockSpec(memory_space=pltpu.HBM)] * len(hbm)
        + [vmem] * len(inputs),
        out_specs=[vmem] * len(outputs),
        out_shape=outputs,
        scratch_shapes=list(scratch),
        cost_estimate=pl.CostEstimate(flops=flops, bytes_accessed=moved, transcendentals=0),
        compiler_params=pltpu.CompilerParams(vmem_limit_bytes=VMEM_LIMIT),
    )(*scalars, *hbm, *inputs)


def turn(value, count):
    eye = (iota((count, count), 0) == iota((count, count), 1)).astype(F32)
    return lax.dot_general(eye, value, (((1,), (1,)), ((), ())), preferred_element_type=F32)


def route_kernel(tokens_hbm, ids_hbm, scores_hbm, swap_hbm, out_ref, ids_ref, scores_ref, swap_ref, sems):
    chosen, rows = ids_ref.shape
    holders = swap_ref.shape[1]
    groups = out_ref.shape[0]
    width = tokens_hbm.shape[1] // groups
    experts = META_COLS
    per_dev = experts // holders
    small = [
        pltpu.make_async_copy(source, target, sems.at[n])
        for n, (source, target) in enumerate(
            ((ids_hbm, ids_ref), (scores_hbm, scores_ref), (swap_hbm, swap_ref))
        )
    ]
    large = [
        pltpu.make_async_copy(
            tokens_hbm.at[:, pl.ds(g * width, width)], out_ref.at[g, :, pl.ds(0, width)], sems.at[3 + g]
        )
        for g in range(groups)
    ]
    for copy in small + large:
        copy.start()
    for copy in small:
        copy.wait()
    ids = turn(ids_ref[...].astype(F32), rows)
    lane = iota((rows, experts), 1)
    hits = [lane.astype(F32) == ids[:, k : k + 1] for k in range(chosen)]
    place = jnp.zeros((rows, experts), F32)
    for k, hit in enumerate(hits):
        place = jnp.where(hit, float(k + 1), place)
    expert = iota((1, experts), 1)
    home = expert // per_dev
    spread = (iota((holders, experts), 1) // per_dev == iota((holders, experts), 0)).astype(F32)
    swap_of = jnp.dot(jnp.broadcast_to(swap_ref[...].astype(F32), (8, holders)), spread, preferred_element_type=F32)
    moved = swap_of[0:1] == (expert % per_dev).astype(F32)
    partner = jnp.where(home + holders // 2 >= holders, home - holders // 2, home + holders // 2)
    holder = jnp.where(moved, partner, home).astype(F32)
    across = jnp.broadcast_to(holder, (experts, experts))
    same = across == across.T
    mate = same & (iota((experts, experts), 0) != iota((experts, experts), 1))
    before = (iota((rows, rows), 1) < iota((rows, rows), 0)).astype(F32)
    ones = (place > 0).astype(F32)
    in_rows = jnp.dot(ones, same.astype(F32), preferred_element_type=F32)
    mate_place = jnp.dot(place, mate.astype(F32), preferred_element_type=F32)
    earlier = ((mate_place > 0) & (mate_place < place)).astype(F32)
    holder_rank = jnp.dot(before, in_rows, preferred_element_type=F32) + earlier
    expert_rank = jnp.dot(before, ones, preferred_element_type=F32)
    kept = (holder_rank < HOLD_CAP) & (expert_rank < CAP_SLOTS)
    code = jnp.where(kept, (CAP_SLOTS * lane).astype(F32) + expert_rank, -1.0)
    scores = scores_ref[...]
    gate = 2.5 * scores / jnp.sum(scores, axis=0, keepdims=True)
    gate_high = gate.astype(BF).astype(F32)
    high = turn(gate_high, rows)
    low = turn((gate - gate_high).astype(BF).astype(F32), rows)
    meta = jnp.zeros((rows, META_COLS), F32)
    for k, hit in enumerate(hits):
        code_k = jnp.sum(jnp.where(hit, code, 0.0), axis=1, keepdims=True)
        meta = jnp.where(lane == k, code_k, meta)
        meta = jnp.where(lane == chosen + k, high[:, k : k + 1], meta)
        meta = jnp.where(lane == 2 * chosen + k, low[:, k : k + 1], meta)
    meta = meta.astype(BF)
    for g in range(groups):
        out_ref[g, :, width:] = meta
    for copy in large:
        copy.wait()


def slot_code(me_ref, index, cells, per_dev, blocks, turn_way):
    unit = blocks * CAP_SLOTS
    cell = index // (per_dev * unit)
    if turn_way:
        cell = me_ref[2] + turn_way * cell
        cell = jnp.where(cell >= cells, cell - cells, jnp.where(cell < 0, cell + cells, cell))
    expert = (me_ref[1] * cells + cell) * per_dev + (index // unit) % per_dev
    return (expert * CAP_SLOTS + index % CAP_SLOTS) + 256 * ((index % unit) // CAP_SLOTS)


def gather_kernel(cells, per_dev, chosen, block_rows, pieces_in, ways, me_ref, *refs):
    pieces, outs = refs[:pieces_in], refs[pieces_in:-2]
    high_ref, low_ref = refs[-2:]
    width = outs[0].shape[1]
    slots = sum(out.shape[0] for out in outs)
    blocks = pieces_in * pieces[0].shape[0] // block_rows
    tok = jnp.concatenate([p[:, :width] for p in pieces], axis=0)
    info = jnp.concatenate([p[:, width:] for p in pieces], axis=0).astype(F32)
    count = tok.shape[0]
    mine = 256.0 * (iota((count, META_COLS), 0) // block_rows).astype(F32)
    keyed = jnp.where(info < 0, -1.0, info + mine)
    turned = keyed.T
    wanted = slot_code(me_ref, iota((slots, 1), 0), cells, per_dev, blocks, ways[0]).astype(F32)
    pick = jnp.zeros((slots, count), F32)
    for k in range(chosen):
        pick = jnp.where(turned[k : k + 1, :] == wanted, 1.0, pick)
    rows = jnp.dot(pick.astype(BF), tok, preferred_element_type=F32).astype(BF)
    each = slots // len(outs)
    for n, out in enumerate(outs):
        out[...] = rows[n * each : (n + 1) * each]
    wanted = slot_code(me_ref, iota((1, slots), 1), cells, per_dev, blocks, ways[1]).astype(F32)
    high = jnp.zeros((count, slots), F32)
    low = jnp.zeros((count, slots), F32)
    for k in range(chosen):
        hit = keyed[:, k : k + 1] == wanted
        high = jnp.where(hit, info[:, chosen + k : chosen + k + 1], high)
        low = jnp.where(hit, info[:, 2 * chosen + k : 2 * chosen + k + 1], low)
    high_ref[...] = high.astype(BF)
    low_ref[...] = low.astype(BF)


def up_kernel(arrivals, me_ref, weight_ref, *refs):
    sources, outs = refs[:arrivals], refs[arrivals:-1]
    rows_ref = refs[-1]
    groups = len(outs)
    cells, per_dev, unit, width = rows_ref.shape
    if arrivals == 1:
        rows_ref = sources[0]
    else:
        for n, source in enumerate(sources):
            rows_ref[n] = source[...].reshape(per_dev, unit, width)
    span = cells // groups
    half = span * unit
    for s in range(per_dev):
        parts = []
        for k in range(groups):
            start = lax.rem(me_ref[0] + groups - k, groups) * span
            parts.append(rows_ref[pl.ds(start, span), s].reshape(half, width))
        rows = jnp.concatenate(parts, axis=0)

        def columns(j, _):
            cols = pl.ds(pl.multiple_of(j * TILE, TILE), TILE)
            result = jnp.dot(rows, weight_ref[s, :, cols], preferred_element_type=F32)
            for k, out in enumerate(outs):
                out[s * half : (s + 1) * half, cols] = result[k * half : (k + 1) * half].astype(out.dtype)
            return 0

        lax.fori_loop(0, weight_ref.shape[2] // TILE, columns, 0)


def down_kernel(groups, arrival_way, me_ref, weight_ref, *refs):
    pieces, outs = refs[:groups], refs[groups:-1]
    rows_ref = refs[-1]
    cells, per_dev, unit, _ = rows_ref.shape
    target = outs[0] if len(outs) == 1 else rows_ref
    span = cells // groups
    half = span * unit
    for s in range(per_dev):
        rows = jnp.concatenate([piece[s * half : (s + 1) * half, :] for piece in pieces], axis=0)

        def columns(j, _):
            cols = pl.ds(pl.multiple_of(j * TILE, TILE), TILE)
            result = jnp.dot(rows, weight_ref[s, :, cols], preferred_element_type=F32).astype(BF)
            for k in range(groups):
                start = lax.rem(me_ref[0] + groups - k, groups) * span
                for n in range(span):
                    index = start + n
                    if arrival_way:
                        index = lax.rem(me_ref[2] + cells - index, cells)
                    else:
                        index = lax.rem(index + cells - me_ref[2], cells)
                    first = k * half + n * unit
                    target[index, s, :, cols] = result[first : first + unit]
            return 0

        lax.fori_loop(0, weight_ref.shape[2] // TILE, columns, 0)
    if len(outs) > 1:
        for n, out in enumerate(outs):
            out[...] = rows_ref[n].reshape(out.shape)


def combine_kernel(arrivals, high_ref, low_ref, *refs):
    sources, outs = refs[:arrivals], refs[arrivals:]
    rows = jnp.concatenate([source[...] for source in sources], axis=0)
    total = jnp.dot(high_ref[...], rows, preferred_element_type=F32)
    total = total + jnp.dot(low_ref[...], rows, preferred_element_type=F32)
    count = outs[0].shape[0]
    for n, out in enumerate(outs):
        out[...] = total[n * count : (n + 1) * count].astype(out.dtype)


def layer(tokens, expert_ids, scores, up_weight, down_weight, swap_slot):
    groups = lax.axis_size("dp")
    planes = lax.axis_size("z")
    cells = lax.axis_size("yc")
    tok_rows, width = tokens.shape
    chosen = expert_ids.shape[1]
    per_dev, part_width, hidden_width = up_weight.shape
    full = part_width + META_COLS
    dp_rows = groups * tok_rows
    me = jnp.stack([lax.axis_index("dp"), lax.axis_index("z"), lax.axis_index("yc")]).astype(I32)

    payload = local_call(
        route_kernel,
        [],
        [jax.ShapeDtypeStruct((groups, tok_rows, full), BF)],
        hbm=[tokens, expert_ids.T, scores.T, swap_slot.reshape(1, -1)],
        scratch=[
            pltpu.VMEM((chosen, tok_rows), I32),
            pltpu.VMEM((chosen, tok_rows), F32),
            pltpu.VMEM((1, swap_slot.shape[0]), I32),
            pltpu.SemaphoreType.DMA((3 + groups,)),
        ],
    )[0]
    own = lax.all_to_all(payload, "dp", 0, 0, tiled=True).reshape(dp_rows, full)
    half = planes // 2
    near = {0: own}
    for offset in (1, -1, half):
        near[offset] = shift(own, "z", offset)
    far = {
        2: shift(near[1], "z", 1),
        -2: shift(near[-1], "z", -1),
        3: shift(near[half], "z", -1),
        -3: shift(near[half], "z", 1),
    }
    unit = len(near) * groups * CAP_SLOTS
    slots = cells * per_dev * unit
    rows_shape = (cells, per_dev, unit, part_width)
    count = slots // groups

    cell_rows = per_dev * unit
    scratch = [pltpu.VMEM(rows_shape, BF)]

    chunks = []
    for n, chunk in enumerate((near, far)):
        tokens_in = [chunk[offset] for offset in chunk]
        one = jax.ShapeDtypeStruct((cell_rows, part_width), BF)
        whole = jax.ShapeDtypeStruct((slots, part_width), BF)
        weights = [jax.ShapeDtypeStruct((len(chunk) * dp_rows, slots), BF)] * 2
        *rows, high, low = local_call(
            functools.partial(
                gather_kernel, cells, per_dev, chosen, tok_rows, len(chunk), (0, -1) if n else (1, 0)
            ),
            tokens_in,
            ([whole] if n else [one] * cells) + weights,
            scalars=(me,),
        )
        if n:
            arrived = lax.all_to_all(rows[0].reshape(cells, cell_rows, part_width), "yc", 0, 0, tiled=True)
            arrived = [arrived.reshape(rows_shape)]
        else:
            arrived = [rows[0]] + [shift(rows[k], "yc", k) for k in range(1, cells)]
        sent = local_call(
            functools.partial(up_kernel, len(arrived)),
            [up_weight] + arrived,
            [jax.ShapeDtypeStruct((count, hidden_width), BF if k else F32) for k in range(groups)],
            scalars=(me,),
            scratch=scratch,
            flops=2 * slots * part_width * hidden_width,
        )
        chunks.append((list(chunk), high, low, sent))
    pieces = []
    for _, _, _, sent in chunks:
        partial = sent[0]
        for k in range(1, groups):
            partial = partial + shift(sent[k], "dp", -k).astype(F32)
        hidden = jax.nn.silu(partial).astype(BF)
        pieces.append([hidden] + [shift(hidden, "dp", k) for k in range(1, groups)])
    total = None
    for n, (offsets, high, low, sent) in enumerate(chunks):
        hidden = pieces[n]
        result = local_call(
            functools.partial(down_kernel, groups, n == 0),
            [down_weight] + hidden,
            [one] * cells if n else [jax.ShapeDtypeStruct(rows_shape, BF)],
            scalars=(me,),
            scratch=scratch,
            flops=2 * slots * part_width * hidden_width,
        )
        if n:
            back = [result[0]] + [shift(result[k], "yc", k) for k in range(1, cells)]
        else:
            back = lax.all_to_all(result[0].reshape(cells, cell_rows, part_width), "yc", 0, 0, tiled=True)
            back = [back.reshape(slots, part_width)]
        sums = local_call(
            functools.partial(combine_kernel, len(back)),
            [high, low] + back,
            [jax.ShapeDtypeStruct((dp_rows, part_width), BF if offset else F32) for offset in offsets],
            flops=4 * slots * part_width * len(offsets) * dp_rows,
        )
        for offset, value in zip(offsets, sums):
            if offset:
                value = shift(value, "z", -offset).astype(F32)
            total = value if total is None else total + value
    parts = total.astype(BF).reshape(groups, tok_rows, part_width)
    parts = lax.all_to_all(parts, "dp", 0, 0, tiled=True)
    return parts.transpose(1, 0, 2).reshape(tok_rows, width)


def solution(mesh):
    groups, holders = mesh.devices.shape
    planes = 8
    grid = Mesh(mesh.devices.reshape(groups, planes, holders // planes), ("dp", "z", "yc"))
    every = ("dp", "z", "yc")
    return jax.shard_map(
        layer,
        mesh=grid,
        in_specs=(
            P(every, None),
            P(every, None),
            P(every, None),
            P(("z", "yc"), "dp", None),
            P(("z", "yc"), None, "dp"),
            P(),
        ),
        out_specs=P(every, None),
        check_vma=False,
    )
```

```python
import functools

import jax
import jax.numpy as jnp
from jax import lax
from jax.experimental import pallas as pl
from jax.experimental.pallas import tpu as pltpu
from jax.sharding import Mesh, PartitionSpec as P

CAP_SLOTS = 2
HOLD_CAP = 3
META_COLS = 128
TILE = 256
WIDE = 1024
COST = 4 << 30
VMEM_LIMIT = 16 << 20
BF = jnp.bfloat16
F32 = jnp.float32
I32 = jnp.int32


def iota(shape, dim):
    return lax.broadcasted_iota(I32, shape, dim)


def shift(value, axis, steps):
    count = lax.axis_size(axis)
    return lax.ppermute(value, axis, [(source, (source + steps) % count) for source in range(count)])


def local_call(kernel, inputs, outputs, scalars=(), hbm=(), scratch=()):
    moved = sum(a.size * a.dtype.itemsize for a in [*hbm, *inputs, *outputs])
    vmem = pl.BlockSpec(memory_space=pltpu.VMEM)
    return pl.pallas_call(
        kernel,
        in_specs=[pl.BlockSpec(memory_space=pltpu.SMEM)] * len(scalars)
        + [pl.BlockSpec(memory_space=pltpu.HBM)] * len(hbm)
        + [vmem] * len(inputs),
        out_specs=[vmem] * len(outputs),
        out_shape=outputs,
        scratch_shapes=list(scratch),
        cost_estimate=pl.CostEstimate(flops=COST, bytes_accessed=moved, transcendentals=0),
        compiler_params=pltpu.CompilerParams(vmem_limit_bytes=VMEM_LIMIT),
    )(*scalars, *hbm, *inputs)


def turn(value, count):
    eye = (iota((count, count), 0) == iota((count, count), 1)).astype(F32)
    return lax.dot_general(eye, value, (((1,), (1,)), ((), ())), preferred_element_type=F32)


def route_kernel(tokens_hbm, ids_hbm, scores_hbm, swap_hbm, out_ref, ids_ref, scores_ref, swap_ref, sems):
    chosen, rows = ids_ref.shape
    holders = swap_ref.shape[1]
    groups = out_ref.shape[0]
    width = tokens_hbm.shape[1] // groups
    experts = META_COLS
    per_dev = experts // holders
    small = [
        pltpu.make_async_copy(source, target, sems.at[n])
        for n, (source, target) in enumerate(
            ((ids_hbm, ids_ref), (scores_hbm, scores_ref), (swap_hbm, swap_ref))
        )
    ]
    large = [
        pltpu.make_async_copy(
            tokens_hbm.at[:, pl.ds(g * width, width)], out_ref.at[g, :, pl.ds(0, width)], sems.at[3 + g]
        )
        for g in range(groups)
    ]
    for copy in small + large:
        copy.start()
    for copy in small:
        copy.wait()
    ids = turn(ids_ref[...].astype(F32), rows)
    lane = iota((rows, experts), 1)
    hits = [lane.astype(F32) == ids[:, k : k + 1] for k in range(chosen)]
    place = jnp.zeros((rows, experts), F32)
    for k, hit in enumerate(hits):
        place = jnp.where(hit, float(k + 1), place)
    expert = iota((1, experts), 1)
    home = expert // per_dev
    spread = (iota((holders, experts), 1) // per_dev == iota((holders, experts), 0)).astype(F32)
    swap_of = jnp.dot(jnp.broadcast_to(swap_ref[...].astype(F32), (8, holders)), spread, preferred_element_type=F32)
    moved = swap_of[0:1] == (expert % per_dev).astype(F32)
    partner = jnp.where(home + holders // 2 >= holders, home - holders // 2, home + holders // 2)
    holder = jnp.where(moved, partner, home).astype(F32)
    across = jnp.broadcast_to(holder, (experts, experts))
    same = across == across.T
    mate = same & (iota((experts, experts), 0) != iota((experts, experts), 1))
    before = (iota((rows, rows), 1) < iota((rows, rows), 0)).astype(F32)
    ones = (place > 0).astype(F32)
    in_rows = jnp.dot(ones, same.astype(F32), preferred_element_type=F32)
    mate_place = jnp.dot(place, mate.astype(F32), preferred_element_type=F32)
    earlier = ((mate_place > 0) & (mate_place < place)).astype(F32)
    holder_rank = jnp.dot(before, in_rows, preferred_element_type=F32) + earlier
    expert_rank = jnp.dot(before, ones, preferred_element_type=F32)
    kept = (holder_rank < HOLD_CAP) & (expert_rank < CAP_SLOTS)
    code = jnp.where(kept, (CAP_SLOTS * lane).astype(F32) + expert_rank, -1.0)
    scores = scores_ref[...]
    gate = 2.5 * scores / jnp.sum(scores, axis=0, keepdims=True)
    gate_high = gate.astype(BF).astype(F32)
    high = turn(gate_high, rows)
    low = turn((gate - gate_high).astype(BF).astype(F32), rows)
    meta = jnp.zeros((rows, META_COLS), F32)
    for k, hit in enumerate(hits):
        code_k = jnp.sum(jnp.where(hit, code, 0.0), axis=1, keepdims=True)
        meta = jnp.where(lane == k, code_k, meta)
        meta = jnp.where(lane == chosen + k, high[:, k : k + 1], meta)
        meta = jnp.where(lane == 2 * chosen + k, low[:, k : k + 1], meta)
    meta = meta.astype(BF)
    for g in range(groups):
        out_ref[g, :, width:] = meta
    for copy in large:
        copy.wait()


def slot_code(me_ref, index, cells, per_dev, blocks, turn_way):
    unit = blocks * CAP_SLOTS
    cell = index // (per_dev * unit)
    if turn_way:
        cell = me_ref[2] + turn_way * cell
        cell = jnp.where(cell >= cells, cell - cells, jnp.where(cell < 0, cell + cells, cell))
    expert = (me_ref[1] * cells + cell) * per_dev + (index // unit) % per_dev
    return (expert * CAP_SLOTS + index % CAP_SLOTS) + 256 * ((index % unit) // CAP_SLOTS)


def keys_of(info, block_rows):
    mine = 256.0 * (iota(info.shape, 0) // block_rows).astype(F32)
    return jnp.where(info < 0, -1.0, info + mine)


def gather_kernel(cells, per_dev, chosen, block_rows, pieces_in, way, me_ref, *refs):
    pieces, outs, info_ref = refs[:pieces_in], refs[pieces_in:-1], refs[-1]
    width = outs[0].shape[1]
    slots = sum(out.shape[0] for out in outs)
    blocks = pieces_in * pieces[0].shape[0] // block_rows
    info = jnp.concatenate([p[:, width:] for p in pieces], axis=0)
    info_ref[...] = info
    count = info.shape[0]
    turned = keys_of(info.astype(F32), block_rows).T
    wanted = slot_code(me_ref, iota((slots, 1), 0), cells, per_dev, blocks, way).astype(F32)
    pick = jnp.zeros((slots, count), F32)
    for k in range(chosen):
        pick = jnp.where(turned[k : k + 1, :] == wanted, 1.0, pick)
    pick = pick.astype(BF)
    each = slots // len(outs)

    def columns(j, _):
        cols = pl.ds(pl.multiple_of(j * TILE, TILE), TILE)
        tok = jnp.concatenate([p[:, cols] for p in pieces], axis=0)
        rows = jnp.dot(pick, tok, preferred_element_type=F32).astype(BF)
        for n, out in enumerate(outs):
            out[:, cols] = rows[n * each : (n + 1) * each]
        return 0

    lax.fori_loop(0, width // TILE, columns, 0)


def mix_kernel(cells, per_dev, chosen, block_rows, way, me_ref, info_ref, high_ref, low_ref):
    count, slots = high_ref.shape
    blocks = count // block_rows
    info = info_ref[...].astype(F32)
    keyed = keys_of(info, block_rows)
    wanted = slot_code(me_ref, iota((1, slots), 1), cells, per_dev, blocks, way).astype(F32)
    high = jnp.zeros((count, slots), F32)
    low = jnp.zeros((count, slots), F32)
    for k in range(chosen):
        hit = keyed[:, k : k + 1] == wanted
        high = jnp.where(hit, info[:, chosen + k : chosen + k + 1], high)
        low = jnp.where(hit, info[:, 2 * chosen + k : 2 * chosen + k + 1], low)
    high_ref[...] = high.astype(BF)
    low_ref[...] = low.astype(BF)


def up_kernel(arrivals, me_ref, weight_ref, *refs):
    sources, outs = refs[:arrivals], refs[arrivals:-1]
    rows_ref = refs[-1]
    groups = len(outs)
    cells, per_dev, unit, width = rows_ref.shape
    if arrivals == 1:
        rows_ref = sources[0]
    else:
        for n, source in enumerate(sources):
            rows_ref[n] = source[...].reshape(per_dev, unit, width)
    span = cells // groups
    half = span * unit
    for s in range(per_dev):
        parts = []
        for k in range(groups):
            start = lax.rem(me_ref[0] + groups - k, groups) * span
            parts.append(rows_ref[pl.ds(start, span), s].reshape(half, width))
        rows = jnp.concatenate(parts, axis=0)

        def columns(j, _):
            cols = pl.ds(pl.multiple_of(j * WIDE, WIDE), WIDE)
            result = jnp.dot(rows, weight_ref[s, :, cols], preferred_element_type=F32)
            for k, out in enumerate(outs):
                out[s * half : (s + 1) * half, cols] = result[k * half : (k + 1) * half].astype(out.dtype)
            return 0

        lax.fori_loop(0, weight_ref.shape[2] // WIDE, columns, 0)


def down_kernel(groups, me_ref, weight_ref, *refs):
    pieces, outs = refs[:groups], refs[groups:-1]
    rows_ref = refs[-1]
    cells, per_dev, unit, _ = rows_ref.shape
    target = outs[0] if len(outs) == 1 else rows_ref
    span = cells // groups
    half = span * unit
    for s in range(per_dev):
        rows = jnp.concatenate([piece[s * half : (s + 1) * half, :] for piece in pieces], axis=0)

        def columns(j, _):
            cols = pl.ds(pl.multiple_of(j * WIDE, WIDE), WIDE)
            result = jnp.dot(rows, weight_ref[s, :, cols], preferred_element_type=F32).astype(BF)
            for k in range(groups):
                start = lax.rem(me_ref[0] + groups - k, groups) * span
                for n in range(span):
                    index = start + n
                    if len(outs) == 1:
                        index = lax.rem(me_ref[2] + cells - index, cells)
                    else:
                        index = lax.rem(index + cells - me_ref[2], cells)
                    first = k * half + n * unit
                    target[index, s, :, cols] = result[first : first + unit]
            return 0

        lax.fori_loop(0, weight_ref.shape[2] // WIDE, columns, 0)
    if len(outs) > 1:
        for n, out in enumerate(outs):
            out[...] = rows_ref[n].reshape(out.shape)


def combine_kernel(arrivals, high_ref, low_ref, *refs):
    sources, outs = refs[:arrivals], refs[arrivals:]
    count = outs[0].shape[0]

    def columns(j, _):
        cols = pl.ds(pl.multiple_of(j * TILE, TILE), TILE)
        rows = jnp.concatenate([source[:, cols] for source in sources], axis=0)
        total = jnp.dot(high_ref[...], rows, preferred_element_type=F32)
        total = total + jnp.dot(low_ref[...], rows, preferred_element_type=F32)
        for n, out in enumerate(outs):
            out[:, cols] = total[n * count : (n + 1) * count].astype(out.dtype)
        return 0

    lax.fori_loop(0, outs[0].shape[1] // TILE, columns, 0)


def layer(tokens, expert_ids, scores, up_weight, down_weight, swap_slot):
    groups = lax.axis_size("dp")
    planes = lax.axis_size("z")
    cells = lax.axis_size("yc")
    tok_rows, width = tokens.shape
    chosen = expert_ids.shape[1]
    per_dev, part_width, hidden_width = up_weight.shape
    full = part_width + META_COLS
    dp_rows = groups * tok_rows
    me = jnp.stack([lax.axis_index("dp"), lax.axis_index("z"), lax.axis_index("yc")]).astype(I32)

    payload = local_call(
        route_kernel,
        [],
        [jax.ShapeDtypeStruct((groups, tok_rows, full), BF)],
        hbm=[tokens, expert_ids.T, scores.T, swap_slot.reshape(1, -1)],
        scratch=[
            pltpu.VMEM((chosen, tok_rows), I32),
            pltpu.VMEM((chosen, tok_rows), F32),
            pltpu.VMEM((1, swap_slot.shape[0]), I32),
            pltpu.SemaphoreType.DMA((3 + groups,)),
        ],
    )[0]
    own = lax.all_to_all(payload, "dp", 0, 0, tiled=True).reshape(dp_rows, full)
    half = planes // 2
    near = {0: own}
    for offset in (1, -1, half):
        near[offset] = shift(own, "z", offset)
    far = {
        2: shift(near[1], "z", 1),
        -2: shift(near[-1], "z", -1),
        3: shift(near[half], "z", -1),
        -3: shift(near[half], "z", 1),
    }
    unit = len(near) * groups * CAP_SLOTS
    slots = cells * per_dev * unit
    rows_shape = (cells, per_dev, unit, part_width)
    count = slots // groups

    cell_rows = per_dev * unit
    scratch = [pltpu.VMEM(rows_shape, BF)]

    chunks = []
    for n, chunk in enumerate((near, far)):
        tokens_in = [chunk[offset] for offset in chunk]
        one = jax.ShapeDtypeStruct((cell_rows, part_width), BF)
        whole = jax.ShapeDtypeStruct((slots, part_width), BF)
        *rows, info = local_call(
            functools.partial(
                gather_kernel, cells, per_dev, chosen, tok_rows, len(chunk), 0 if n else 1
            ),
            tokens_in,
            ([whole] if n else [one] * cells)
            + [jax.ShapeDtypeStruct((len(chunk) * dp_rows, META_COLS), BF)],
            scalars=(me,),
        )
        if n:
            arrived = lax.all_to_all(rows[0].reshape(cells, cell_rows, part_width), "yc", 0, 0, tiled=True)
            arrived = [arrived.reshape(rows_shape)]
        else:
            arrived = [rows[0]] + [shift(rows[k], "yc", k) for k in range(1, cells)]
        sent = local_call(
            functools.partial(up_kernel, len(arrived)),
            [up_weight] + arrived,
            [jax.ShapeDtypeStruct((count, hidden_width), BF if k else F32) for k in range(groups)],
            scalars=(me,),
            scratch=scratch,
        )
        high, low = local_call(
            functools.partial(mix_kernel, cells, per_dev, chosen, tok_rows, -n),
            [info],
            [jax.ShapeDtypeStruct((len(chunk) * dp_rows, slots), BF)] * 2,
            scalars=(me,),
        )
        chunks.append((list(chunk), high, low, sent))
    pieces = []
    for _, _, _, sent in chunks:
        partial = sent[0]
        for k in range(1, groups):
            partial = partial + shift(sent[k], "dp", -k).astype(F32)
        hidden = jax.nn.silu(partial).astype(BF)
        pieces.append([hidden] + [shift(hidden, "dp", k) for k in range(1, groups)])
    total = None
    for n, (offsets, high, low, sent) in enumerate(chunks):
        hidden = pieces[n]
        result = local_call(
            functools.partial(down_kernel, groups),
            [down_weight] + hidden,
            [one] * cells if n else [jax.ShapeDtypeStruct(rows_shape, BF)],
            scalars=(me,),
            scratch=scratch,
        )
        if n:
            back = [result[0]] + [shift(result[k], "yc", k) for k in range(1, cells)]
        else:
            back = lax.all_to_all(result[0].reshape(cells, cell_rows, part_width), "yc", 0, 0, tiled=True)
            back = [back.reshape(slots, part_width)]
        sums = local_call(
            functools.partial(combine_kernel, len(back)),
            [high, low] + back,
            [jax.ShapeDtypeStruct((dp_rows, part_width), F32 if offset in (0, 2, -2) else BF) for offset in offsets],
        )
        sums = dict(zip(offsets, sums))
        if n:
            for way in (1, -1):
                passed = shift(sums[3 * way], "z", -way).astype(F32) + sums[2 * way]
                total = total + shift(passed.astype(BF), "z", -2 * way).astype(F32)
        else:
            total = sums[0]
            for offset in offsets[1:]:
                total = total + shift(sums[offset], "z", -offset).astype(F32)
    parts = total.astype(BF).reshape(groups, tok_rows, part_width)
    parts = lax.all_to_all(parts, "dp", 0, 0, tiled=True)
    return parts.transpose(1, 0, 2).reshape(tok_rows, width)


def solution(mesh):
    groups, holders = mesh.devices.shape
    planes = 8
    grid = Mesh(mesh.devices.reshape(groups, planes, holders // planes), ("dp", "z", "yc"))
    every = ("dp", "z", "yc")
    return jax.shard_map(
        layer,
        mesh=grid,
        in_specs=(
            P(every, None),
            P(every, None),
            P(every, None),
            P(("z", "yc"), "dp", None),
            P(("z", "yc"), None, "dp"),
            P(),
        ),
        out_specs=P(every, None),
        check_vma=False,
    )
```

```python
import functools

import jax
import jax.numpy as jnp
from jax import lax
from jax.experimental import pallas as pl
from jax.experimental.pallas import tpu as pltpu
from jax.sharding import Mesh, PartitionSpec as P

CAP_SLOTS = 2
HOLD_CAP = 3
META_COLS = 128
TILE = 256
WIDE = 1024
COST = 4 << 30
VMEM_LIMIT = 16 << 20
BF = jnp.bfloat16
F32 = jnp.float32
I32 = jnp.int32


def iota(shape, dim):
    return lax.broadcasted_iota(I32, shape, dim)


def shift(value, axis, steps):
    count = lax.axis_size(axis)
    return lax.ppermute(value, axis, [(source, (source + steps) % count) for source in range(count)])


def local_call(kernel, inputs, outputs, scalars=(), hbm=(), scratch=()):
    moved = sum(a.size * a.dtype.itemsize for a in [*hbm, *inputs, *outputs])
    vmem = pl.BlockSpec(memory_space=pltpu.VMEM)
    return pl.pallas_call(
        kernel,
        in_specs=[pl.BlockSpec(memory_space=pltpu.SMEM)] * len(scalars)
        + [pl.BlockSpec(memory_space=pltpu.HBM)] * len(hbm)
        + [vmem] * len(inputs),
        out_specs=[vmem] * len(outputs),
        out_shape=outputs,
        scratch_shapes=list(scratch),
        cost_estimate=pl.CostEstimate(flops=COST, bytes_accessed=moved, transcendentals=0),
        compiler_params=pltpu.CompilerParams(vmem_limit_bytes=VMEM_LIMIT),
    )(*scalars, *hbm, *inputs)


def turn(value, count):
    eye = (iota((count, count), 0) == iota((count, count), 1)).astype(F32)
    return lax.dot_general(eye, value, (((1,), (1,)), ((), ())), preferred_element_type=F32)


def route_kernel(tokens_hbm, ids_hbm, scores_hbm, swap_hbm, out_ref, ids_ref, scores_ref, swap_ref, sems):
    chosen, rows = ids_ref.shape
    holders = swap_ref.shape[1]
    groups = out_ref.shape[0]
    width = tokens_hbm.shape[1] // groups
    experts = META_COLS
    per_dev = experts // holders
    small = [
        pltpu.make_async_copy(source, target, sems.at[n])
        for n, (source, target) in enumerate(
            ((ids_hbm, ids_ref), (scores_hbm, scores_ref), (swap_hbm, swap_ref))
        )
    ]
    large = [
        pltpu.make_async_copy(
            tokens_hbm.at[:, pl.ds(g * width, width)], out_ref.at[g, :, pl.ds(0, width)], sems.at[3 + g]
        )
        for g in range(groups)
    ]
    for copy in small + large:
        copy.start()
    for copy in small:
        copy.wait()
    ids = turn(ids_ref[...].astype(F32), rows)
    lane = iota((rows, experts), 1)
    hits = [lane.astype(F32) == ids[:, k : k + 1] for k in range(chosen)]
    place = jnp.zeros((rows, experts), F32)
    for k, hit in enumerate(hits):
        place = jnp.where(hit, float(k + 1), place)
    expert = iota((1, experts), 1)
    home = expert // per_dev
    spread = (iota((holders, experts), 1) // per_dev == iota((holders, experts), 0)).astype(F32)
    swap_of = jnp.dot(jnp.broadcast_to(swap_ref[...].astype(F32), (8, holders)), spread, preferred_element_type=F32)
    moved = swap_of[0:1] == (expert % per_dev).astype(F32)
    partner = jnp.where(home + holders // 2 >= holders, home - holders // 2, home + holders // 2)
    holder = jnp.where(moved, partner, home).astype(F32)
    across = jnp.broadcast_to(holder, (experts, experts))
    same = across == across.T
    mate = same & (iota((experts, experts), 0) != iota((experts, experts), 1))
    before = (iota((rows, rows), 1) < iota((rows, rows), 0)).astype(F32)
    ones = (place > 0).astype(F32)
    in_rows = jnp.dot(ones, same.astype(F32), preferred_element_type=F32)
    mate_place = jnp.dot(place, mate.astype(F32), preferred_element_type=F32)
    earlier = ((mate_place > 0) & (mate_place < place)).astype(F32)
    holder_rank = jnp.dot(before, in_rows, preferred_element_type=F32) + earlier
    expert_rank = jnp.dot(before, ones, preferred_element_type=F32)
    kept = (holder_rank < HOLD_CAP) & (expert_rank < CAP_SLOTS)
    code = jnp.where(kept, (CAP_SLOTS * lane).astype(F32) + expert_rank, -1.0)
    scores = scores_ref[...]
    gate = 2.5 * scores / jnp.sum(scores, axis=0, keepdims=True)
    gate_high = gate.astype(BF).astype(F32)
    high = turn(gate_high, rows)
    low = turn((gate - gate_high).astype(BF).astype(F32), rows)
    meta = jnp.zeros((rows, META_COLS), F32)
    for k, hit in enumerate(hits):
        code_k = jnp.sum(jnp.where(hit, code, 0.0), axis=1, keepdims=True)
        meta = jnp.where(lane == k, code_k, meta)
        meta = jnp.where(lane == chosen + k, high[:, k : k + 1], meta)
        meta = jnp.where(lane == 2 * chosen + k, low[:, k : k + 1], meta)
    meta = meta.astype(BF)
    for g in range(groups):
        out_ref[g, :, width:] = meta
    for copy in large:
        copy.wait()


def slot_code(me_ref, index, cells, per_dev, blocks, turn_way):
    unit = blocks * CAP_SLOTS
    cell = index // (per_dev * unit)
    if turn_way:
        cell = me_ref[2] + turn_way * cell
        cell = jnp.where(cell >= cells, cell - cells, jnp.where(cell < 0, cell + cells, cell))
    expert = (me_ref[1] * cells + cell) * per_dev + (index // unit) % per_dev
    return (expert * CAP_SLOTS + index % CAP_SLOTS) + 256 * ((index % unit) // CAP_SLOTS)


def keys_of(info, block_rows):
    mine = 256.0 * (iota(info.shape, 0) // block_rows).astype(F32)
    return jnp.where(info < 0, -1.0, info + mine)


def gather_kernel(cells, per_dev, chosen, block_rows, pieces_in, way, me_ref, *refs):
    pieces, outs, info_ref = refs[:pieces_in], refs[pieces_in:-1], refs[-1]
    width = outs[0].shape[1]
    slots = sum(out.shape[0] for out in outs)
    blocks = pieces_in * pieces[0].shape[0] // block_rows
    info = jnp.concatenate([p[:, width:] for p in pieces], axis=0)
    info_ref[...] = info
    count = info.shape[0]
    turned = keys_of(info.astype(F32), block_rows).T
    wanted = slot_code(me_ref, iota((slots, 1), 0), cells, per_dev, blocks, way).astype(F32)
    pick = jnp.zeros((slots, count), F32)
    for k in range(chosen):
        pick = jnp.where(turned[k : k + 1, :] == wanted, 1.0, pick)
    pick = pick.astype(BF)
    each = slots // len(outs)

    def columns(j, _):
        cols = pl.ds(pl.multiple_of(j * TILE, TILE), TILE)
        tok = jnp.concatenate([p[:, cols] for p in pieces], axis=0)
        rows = jnp.dot(pick, tok, preferred_element_type=F32).astype(BF)
        for n, out in enumerate(outs):
            out[:, cols] = rows[n * each : (n + 1) * each]
        return 0

    lax.fori_loop(0, width // TILE, columns, 0)


def mix_kernel(cells, per_dev, chosen, block_rows, way, me_ref, info_ref, high_ref, low_ref):
    count, slots = high_ref.shape
    blocks = count // block_rows
    info = info_ref[...].astype(F32)
    keyed = keys_of(info, block_rows)
    wanted = slot_code(me_ref, iota((1, slots), 1), cells, per_dev, blocks, way).astype(F32)
    high = jnp.zeros((count, slots), F32)
    low = jnp.zeros((count, slots), F32)
    for k in range(chosen):
        hit = keyed[:, k : k + 1] == wanted
        high = jnp.where(hit, info[:, chosen + k : chosen + k + 1], high)
        low = jnp.where(hit, info[:, 2 * chosen + k : 2 * chosen + k + 1], low)
    high_ref[...] = high.astype(BF)
    low_ref[...] = low.astype(BF)


def up_kernel(arrivals, me_ref, weight_ref, *refs):
    sources, outs = refs[:arrivals], refs[arrivals:-1]
    rows_ref = refs[-1]
    groups = len(outs)
    cells, per_dev, unit, width = rows_ref.shape
    if arrivals == 1:
        rows_ref = sources[0]
    else:
        for n, source in enumerate(sources):
            rows_ref[n] = source[...].reshape(per_dev, unit, width)
    span = cells // groups
    half = span * unit
    for s in range(per_dev):
        parts = []
        for k in range(groups):
            start = lax.rem(me_ref[0] + groups - k, groups) * span
            parts.append(rows_ref[pl.ds(start, span), s].reshape(half, width))
        rows = jnp.concatenate(parts, axis=0)

        def columns(j, _):
            cols = pl.ds(pl.multiple_of(j * WIDE, WIDE), WIDE)
            result = jnp.dot(rows, weight_ref[s, :, cols], preferred_element_type=F32)
            for k, out in enumerate(outs):
                out[s * half : (s + 1) * half, cols] = result[k * half : (k + 1) * half].astype(out.dtype)
            return 0

        lax.fori_loop(0, weight_ref.shape[2] // WIDE, columns, 0)


def down_kernel(groups, me_ref, weight_ref, *refs):
    pieces, outs = refs[:groups], refs[groups:-1]
    rows_ref = refs[-1]
    cells, per_dev, unit, _ = rows_ref.shape
    target = outs[0] if len(outs) == 1 else rows_ref
    span = cells // groups
    half = span * unit
    for s in range(per_dev):
        rows = jnp.concatenate([piece[s * half : (s + 1) * half, :] for piece in pieces], axis=0)

        def columns(j, _):
            cols = pl.ds(pl.multiple_of(j * WIDE, WIDE), WIDE)
            result = jnp.dot(rows, weight_ref[s, :, cols], preferred_element_type=F32).astype(BF)
            for k in range(groups):
                start = lax.rem(me_ref[0] + groups - k, groups) * span
                for n in range(span):
                    index = start + n
                    if len(outs) == 1:
                        index = lax.rem(me_ref[2] + cells - index, cells)
                    else:
                        index = lax.rem(index + cells - me_ref[2], cells)
                    first = k * half + n * unit
                    target[index, s, :, cols] = result[first : first + unit]
            return 0

        lax.fori_loop(0, weight_ref.shape[2] // WIDE, columns, 0)
    if len(outs) > 1:
        for n, out in enumerate(outs):
            out[...] = rows_ref[n].reshape(out.shape)


def combine_kernel(arrivals, high_ref, low_ref, *refs):
    sources, outs = refs[:arrivals], refs[arrivals:]
    count = outs[0].shape[0]

    def columns(j, _):
        cols = pl.ds(pl.multiple_of(j * TILE, TILE), TILE)
        rows = jnp.concatenate([source[:, cols] for source in sources], axis=0)
        total = jnp.dot(high_ref[...], rows, preferred_element_type=F32)
        total = total + jnp.dot(low_ref[...], rows, preferred_element_type=F32)
        for n, out in enumerate(outs):
            out[:, cols] = total[n * count : (n + 1) * count].astype(out.dtype)
        return 0

    lax.fori_loop(0, outs[0].shape[1] // TILE, columns, 0)


def layer(tokens, expert_ids, scores, up_weight, down_weight, swap_slot):
    groups = lax.axis_size("dp")
    planes = lax.axis_size("z")
    cells = lax.axis_size("yc")
    tok_rows, width = tokens.shape
    chosen = expert_ids.shape[1]
    per_dev, part_width, hidden_width = up_weight.shape
    full = part_width + META_COLS
    dp_rows = groups * tok_rows
    me = jnp.stack([lax.axis_index("dp"), lax.axis_index("z"), lax.axis_index("yc")]).astype(I32)

    payload = local_call(
        route_kernel,
        [],
        [jax.ShapeDtypeStruct((groups, tok_rows, full), BF)],
        hbm=[tokens, expert_ids.T, scores.T, swap_slot.reshape(1, -1)],
        scratch=[
            pltpu.VMEM((chosen, tok_rows), I32),
            pltpu.VMEM((chosen, tok_rows), F32),
            pltpu.VMEM((1, swap_slot.shape[0]), I32),
            pltpu.SemaphoreType.DMA((3 + groups,)),
        ],
    )[0]
    own = lax.all_to_all(payload, "dp", 0, 0, tiled=True).reshape(dp_rows, full)
    half = planes // 2
    near = {0: own}
    for offset in (1, -1, half):
        near[offset] = shift(own, "z", offset)
    far = {
        2: shift(near[1], "z", 1),
        -2: shift(near[-1], "z", -1),
        3: shift(near[half], "z", -1),
        -3: shift(near[half], "z", 1),
    }
    unit = len(near) * groups * CAP_SLOTS
    slots = cells * per_dev * unit
    rows_shape = (cells, per_dev, unit, part_width)
    count = slots // groups

    cell_rows = per_dev * unit
    scratch = [pltpu.VMEM(rows_shape, BF)]

    chunks = []
    for n, chunk in enumerate((near, far)):
        tokens_in = [chunk[offset] for offset in chunk]
        one = jax.ShapeDtypeStruct((cell_rows, part_width), BF)
        whole = jax.ShapeDtypeStruct((slots, part_width), BF)
        *rows, info = local_call(
            functools.partial(
                gather_kernel, cells, per_dev, chosen, tok_rows, len(chunk), 0 if n else 1
            ),
            tokens_in,
            ([whole] if n else [one] * cells)
            + [jax.ShapeDtypeStruct((len(chunk) * dp_rows, META_COLS), BF)],
            scalars=(me,),
        )
        if n:
            arrived = lax.all_to_all(rows[0].reshape(cells, cell_rows, part_width), "yc", 0, 0, tiled=True)
            arrived = [arrived.reshape(rows_shape)]
        else:
            arrived = [rows[0]] + [shift(rows[k], "yc", k) for k in range(1, cells)]
        sent = local_call(
            functools.partial(up_kernel, len(arrived)),
            [up_weight] + arrived,
            [jax.ShapeDtypeStruct((count, hidden_width), BF if k else F32) for k in range(groups)],
            scalars=(me,),
            scratch=scratch,
        )
        high, low = local_call(
            functools.partial(mix_kernel, cells, per_dev, chosen, tok_rows, -n),
            [info],
            [jax.ShapeDtypeStruct((len(chunk) * dp_rows, slots), BF)] * 2,
            scalars=(me,),
        )
        chunks.append((list(chunk), high, low, sent))
    pieces = []
    for _, _, _, sent in chunks:
        partial = sent[0]
        for k in range(1, groups):
            partial = partial + shift(sent[k], "dp", -k).astype(F32)
        hidden = jax.nn.silu(partial).astype(BF)
        pieces.append([hidden] + [shift(hidden, "dp", k) for k in range(1, groups)])
    total = None
    for n, (offsets, high, low, sent) in enumerate(chunks):
        hidden = pieces[n]
        result = local_call(
            functools.partial(down_kernel, groups),
            [down_weight] + hidden,
            [one] * cells if n else [jax.ShapeDtypeStruct(rows_shape, BF)],
            scalars=(me,),
            scratch=scratch,
        )
        if n:
            back = [result[0]] + [shift(result[k], "yc", k) for k in range(1, cells)]
        else:
            back = lax.all_to_all(result[0].reshape(cells, cell_rows, part_width), "yc", 0, 0, tiled=True)
            back = [back.reshape(slots, part_width)]
        sums = local_call(
            functools.partial(combine_kernel, len(back)),
            [high, low] + back,
            [jax.ShapeDtypeStruct((dp_rows, part_width), BF if offset else F32) for offset in offsets],
        )
        sums = dict(zip(offsets, sums))
        if n:
            for offset in offsets:
                total = total + shift(sums[offset], "z", -offset).astype(F32)
        else:
            total = sums[0]
            for offset in offsets[1:]:
                total = total + shift(sums[offset], "z", -offset).astype(F32)
    parts = total.astype(BF).reshape(groups, tok_rows, part_width)
    parts = lax.all_to_all(parts, "dp", 0, 0, tiled=True)
    return parts.transpose(1, 0, 2).reshape(tok_rows, width)


def solution(mesh):
    groups, holders = mesh.devices.shape
    planes = 8
    grid = Mesh(mesh.devices.reshape(groups, planes, holders // planes), ("dp", "z", "yc"))
    every = ("dp", "z", "yc")
    return jax.shard_map(
        layer,
        mesh=grid,
        in_specs=(
            P(every, None),
            P(every, None),
            P(every, None),
            P(("z", "yc"), "dp", None),
            P(("z", "yc"), None, "dp"),
            P(),
        ),
        out_specs=P(every, None),
        check_vma=False,
    )
```
